128 devices in a mesh: grp: 8 (over z_lo, y), pen: 16 (over z_hi, x, core).
Axes of the slice: x: 4, y: 4, z: 4 (z_hi: 2, z_lo: 2; z = z_hi * 2 + z_lo), core: 2. Of those that a mesh axis runs over, the one named last changes fastest.
Arguments:
- columns: float32 [2, 512, 512, 512], P(None, 'grp', 'pen'), may hold values from -6 to 6
- basis_in_x: float32 [512, 512], replicated, may hold values from -0.25 to 0.25
- basis_in_y: float32 [512, 512], replicated, may hold values from -0.25 to 0.25
- basis_in_z: float32 [512, 512], replicated, may hold values from -0.25 to 0.25
- basis_out_x: float32 [512, 512], replicated, may hold values from -0.25 to 0.25
- basis_out_y: float32 [512, 512], replicated, may hold values from -0.25 to 0.25
- basis_out_z: float32 [512, 512], replicated, may hold values from -0.25 to 0.25
- eig_x: float32 [512], replicated, may hold values from 0.05 to 3
- eig_y: float32 [512], replicated, may hold values from 0.05 to 3
- eig_z: float32 [512], replicated, may hold values from 0.05 to 3
- shift_table: float32 [64], replicated, may hold values from 0.5 to 8
- shift_index: int32 [2], replicated, may hold values from 0 to 63
Outputs:
- solved: float32 [2, 512, 512, 512], P(None, 'grp', 'pen')
The draws below stay inside these ranges and needn't reach their ends.
Inputs may be any that keep to these rules, and one draw needn't show every extreme that they name: `shift_index`: indices into shift_table.
All inputs are finite; a program needn't handle non-finite values.
Results may differ from the reference program's by a relative error of at most 0.00007.
Values sent between devices are 32-bit elements; how exact they have to be, the bound alone decides.
A program may use at most 192 MiB of HBM per device.

```python
import math
import jax
import jax.numpy as jnp
from jax import lax

N = 512
COLS = 2
NSHIFT = 64


def shard_levels(key, dims, pieces, low, largest):
    def one(position, blocks):
        draws = jax.random.uniform(jax.random.fold_in(jax.random.fold_in(key, 6), position), (blocks,), jnp.float32, low / len(pieces), largest / len(pieces))
        return jnp.repeat(jnp.exp(draws), dims[position] // blocks).reshape((-1,) + (1,) * (len(dims) - position - 1))

    loudness = one(*pieces[0])
    for cut in pieces[1:]:
        loudness = loudness * one(*cut)
    return loudness


def centred(stream_key, shape, spread, bound, cuts=(), kind=jnp.bfloat16):
    level = shard_levels(stream_key, shape, cuts, -0.22, 0.18) if cuts else 1.0
    values = jax.random.normal(stream_key, shape, jnp.float32) * spread * level
    return jnp.minimum(jnp.maximum(values, -bound), bound).astype(kind)


def setup_inputs(seed: int = 0) -> dict:
    keys = jax.random.split(jax.random.key(seed), 13)
    return {
        "columns": centred(keys[0], (COLS, N, N, N), 1.0, 6.0, ((1, 8), (2, 16)), jnp.float32),
        "basis_in_x": centred(keys[1], (N, N), N ** -0.5, 0.25, (), jnp.float32),
        "basis_in_y": centred(keys[2], (N, N), N ** -0.5, 0.25, (), jnp.float32),
        "basis_in_z": centred(keys[3], (N, N), N ** -0.5, 0.25, (), jnp.float32),
        "basis_out_x": centred(keys[4], (N, N), N ** -0.5, 0.25, (), jnp.float32),
        "basis_out_y": centred(keys[5], (N, N), N ** -0.5, 0.25, (), jnp.float32),
        "basis_out_z": centred(keys[6], (N, N), N ** -0.5, 0.25, (), jnp.float32),
        "eig_x": jnp.clip(jnp.exp(jax.random.uniform(keys[7], (N,), jnp.float32, math.log(0.05), math.log(3.0))), 0.05, 3.0),
        "eig_y": jnp.clip(jnp.exp(jax.random.uniform(keys[8], (N,), jnp.float32, math.log(0.05), math.log(3.0))), 0.05, 3.0),
        "eig_z": jnp.clip(jnp.exp(jax.random.uniform(keys[9], (N,), jnp.float32, math.log(0.05), math.log(3.0))), 0.05, 3.0),
        "shift_table": jnp.clip(jnp.exp(jax.random.uniform(keys[10], (NSHIFT,), jnp.float32, math.log(0.5), math.log(8.0))), 0.5, 8.0),
        "shift_index": jax.random.randint(keys[11], (COLS,), 0, NSHIFT).astype(jnp.int32),
    }


def reference(columns, basis_in_x, basis_in_y, basis_in_z, basis_out_x, basis_out_y, basis_out_z, eig_x, eig_y, eig_z, shift_table, shift_index):
    highest = lax.Precision.HIGHEST
    shift_values = shift_table[shift_index]
    eig_sum = eig_x[:, None, None] + eig_y[None, :, None] + eig_z[None, None, :]

    def solve_one(pair):
        column, shift_value = pair
        scaling = jnp.sqrt(2.0 * shift_value)
        spectral = jnp.einsum('ix,xyz->iyz', basis_in_x, column, precision=highest)
        spectral = jnp.einsum('jy,iyz->ijz', basis_in_y, spectral, precision=highest)
        spectral = jnp.einsum('kz,ijz->ijk', basis_in_z, spectral, precision=highest)
        scaled = scaling * spectral / (eig_sum + shift_value)
        result = jnp.einsum('xi,ijk->xjk', basis_out_x, scaled, precision=highest)
        result = jnp.einsum('yj,xjk->xyk', basis_out_y, result, precision=highest)
        result = jnp.einsum('zk,xyk->xyz', basis_out_z, result, precision=highest)
        return result
    return lax.map(solve_one, (columns, shift_values))
```

```python
import jax
import jax.numpy as jnp
from jax import lax
from jax.experimental import pallas as pl
from jax.experimental.pallas import tpu as pltpu
from jax.sharding import PartitionSpec as P

MESH = pl.DeviceIdType.MESH


def exchange_kernel(x_ref, o_ref, send_sem, recv_sem, local_sem):
    grp_count, pen_count = lax.axis_size("grp"), lax.axis_size("pen")
    count = grp_count * pen_count
    steps = x_ref.shape[1]
    me = lax.axis_index("grp") * pen_count + lax.axis_index("pen")

    def place(t):
        return {"grp": t // pen_count, "pen": t % pen_count}

    barrier = pltpu.get_barrier_semaphore()

    def greet(i, carry):
        pl.semaphore_signal(
            barrier, inc=1, device_id=place((me + i) % count), device_id_type=MESH
        )
        return carry

    lax.fori_loop(1, count, greet, 0)
    pl.semaphore_wait(barrier, count - 1)

    def one_step(s, carry):
        def send(i, inner):
            t = (me + i) % count
            pltpu.make_async_remote_copy(
                src_ref=x_ref.at[t, s],
                dst_ref=o_ref.at[me, s],
                send_sem=send_sem,
                recv_sem=recv_sem,
                device_id=place(t),
                device_id_type=MESH,
            ).start()
            return inner

        return lax.fori_loop(1, count, send, carry)

    own = pltpu.make_async_copy(x_ref.at[me], o_ref.at[me], local_sem)
    own.start()
    lax.fori_loop(0, steps, one_step, 0)
    own.wait()
    others = pl.ds(0, count - 1)
    pltpu.make_async_copy(x_ref.at[others], x_ref.at[others], send_sem).wait()
    pltpu.make_async_copy(o_ref.at[others], o_ref.at[others], recv_sem).wait()


def exchange(x):
    return pl.pallas_call(
        exchange_kernel,
        out_shape=jax.ShapeDtypeStruct(x.shape, x.dtype),
        in_specs=[pl.BlockSpec(memory_space=pl.ANY)],
        out_specs=pl.BlockSpec(memory_space=pl.ANY),
        scratch_shapes=[pltpu.SemaphoreType.DMA] * 3,
        compiler_params=pltpu.CompilerParams(collective_id=0, has_side_effects=True),
        name="exchange",
    )(x)


def per_device(
    columns,
    basis_in_x,
    basis_in_y,
    basis_in_z,
    basis_out_x,
    basis_out_y,
    basis_out_z,
    eig_x,
    eig_y,
    eig_z,
    shift_table,
    shift_index,
):
    high = lax.Precision.HIGH
    shift_values = shift_table[shift_index]
    count, x_local, y_local, length = columns.shape
    pen_count = lax.axis_size("pen")
    grp_count = lax.axis_size("grp")
    devices = pen_count * grp_count
    z_slab = length // devices
    rows = x_local * y_local // 128
    forward = jnp.einsum("kz,cxyz->kcxy", basis_in_z, columns, precision=high)
    forward = forward.reshape(devices, z_slab * count, rows, 128)
    planes = exchange(forward)
    planes = planes.reshape(grp_count, pen_count, z_slab, count, x_local, y_local)
    planes = planes.transpose(3, 2, 0, 4, 1, 5).reshape(count, z_slab, length, length)
    spectral = jnp.einsum("ix,ckxy->ckiy", basis_in_x, planes, precision=high)
    spectral = jnp.einsum("jy,ckiy->ckij", basis_in_y, spectral, precision=high)
    start_row = (lax.axis_index("grp") * pen_count + lax.axis_index("pen")) * z_slab
    eig_z_part = lax.dynamic_slice_in_dim(eig_z, start_row, z_slab)
    shift_wide = shift_values[:, None, None, None]
    denominator = (
        eig_z_part[None, :, None, None]
        + eig_x[None, None, :, None]
        + eig_y[None, None, None, :]
        + shift_wide
    )
    scaled = jnp.sqrt(2.0 * shift_wide) * spectral / denominator
    back = jnp.einsum("xi,ckij->ckxj", basis_out_x, scaled, precision=high)
    back = jnp.einsum("yj,ckxj->ckxy", basis_out_y, back, precision=high)
    back = back.reshape(count, z_slab, grp_count, x_local, pen_count, y_local)
    back = back.transpose(2, 4, 1, 0, 3, 5).reshape(devices, z_slab * count, rows, 128)
    returned = exchange(back)
    returned = returned.reshape(length, count, x_local, y_local)
    return jnp.einsum("zk,kcxy->cxyz", basis_out_z, returned, precision=high)


def solution(mesh):
    in_specs = (P(None, "grp", "pen", None), P(), P(), P(), P(), P(), P(), P(), P(), P(), P(), P())
    out_specs = P(None, "grp", "pen", None)
    return jax.shard_map(
        per_device, mesh=mesh, in_specs=in_specs, out_specs=out_specs, check_vma=False
    )
```

```python
import jax
import jax.numpy as jnp
from jax import lax
from jax.experimental import pallas as pl
from jax.experimental.pallas import tpu as pltpu
from jax.sharding import PartitionSpec as P

MESH = pl.DeviceIdType.MESH
F32, BF16 = jnp.float32, jnp.bfloat16
NT = (((1,), (1,)), ((), ()))
NN = (((1,), (0,)), ((), ()))
LANES = 128


def split(value):
    high = value.astype(BF16)
    return high, (value - high.astype(F32)).astype(BF16)


def product(left, right, dims):
    def dot(a, b):
        return lax.dot_general(a, b, dims, preferred_element_type=F32)

    return dot(left[0], right[0]) + dot(left[1], right[0]) + dot(left[0], right[1])


def solve_kernel(
    shift_index,
    shift_table,
    eig_z,
    eig_x,
    eig_y,
    columns,
    basis_in_x,
    basis_in_y,
    basis_in_z,
    basis_out_x,
    basis_out_y,
    basis_out_z,
    solved,
    cube,
    lines_high,
    lines_low,
    send_there,
    planes,
    send_back,
    returned,
    stacked,
    bases_high,
    bases_low,
    first_high,
    first_low,
    second_high,
    second_low,
    eig_sum,
    load_sem,
    store_sem,
    own_there_sem,
    own_back_sem,
    there_sem,
    back_sem,
    there_recv,
    back_recv,
):
    grp_count, pen_count = lax.axis_size("grp"), lax.axis_size("pen")
    count = grp_count * pen_count
    cols, cells, length = columns.shape
    slots = length // count
    steps = cols * slots
    rows = cells // LANES
    y_local = length // pen_count
    x_local = length // grp_count
    me = lax.axis_index("grp") * pen_count + lax.axis_index("pen")

    def place(t):
        return {"grp": t // pen_count, "pen": t % pen_count}

    bases = (basis_in_z, basis_in_y, basis_in_x, basis_out_x, basis_out_y, basis_out_z)
    lane_parts = length // LANES

    def base_part(b, part):
        return pltpu.make_async_copy(
            bases[b].at[:, pl.ds(part * LANES, LANES)],
            send_back.at[b, pl.ds(part * length, length), :],
            load_sem.at[cols + b],
        )

    def column_load(c, part):
        lanes = pl.ds(part * LANES, LANES)
        return pltpu.make_async_copy(columns.at[c, :, lanes], cube.at[c, part], load_sem.at[c])

    def column_wait(c):
        pltpu.make_async_copy(cube.at[c], cube.at[c], load_sem.at[c]).wait()

    for part in range(lane_parts):
        base_part(0, part).start()
    for c in range(cols):
        for part in range(lane_parts):
            column_load(c, part).start()
    for b in range(1, len(bases)):
        for part in range(lane_parts):
            base_part(b, part).start()

    barrier = pltpu.get_barrier_semaphore()

    def greet(i, carry):
        pl.semaphore_signal(
            barrier, inc=1, device_id=place((me + i) % count), device_id_type=MESH
        )
        return carry

    lax.fori_loop(1, count, greet, 0)

    def base_wait(b):
        whole = send_back.at[b]
        pltpu.make_async_copy(whole, whole, load_sem.at[cols + b]).wait()

    base_wait(0)
    for part in range(lane_parts):
        for slot in range(slots):
            start = part * length + slot * count
            high, low = split(send_back[0, start : start + count, :])
            lanes = slice(part * LANES, (part + 1) * LANES)
            stacked[2 * slot * count : (2 * slot + 1) * count, lanes] = high
            stacked[(2 * slot + 1) * count : (2 * slot + 2) * count, lanes] = low

    def prepare(c):
        def one(y, carry):
            to = pl.ds(
                pl.multiple_of((y % rows) * LANES + (y // rows) * x_local, x_local), x_local
            )
            for part in range(lane_parts):
                here = cube[c, part, pl.ds(y, x_local, stride=y_local), :]
                lanes = slice(part * LANES, (part + 1) * LANES)
                lines_high[to, lanes], lines_low[to, lanes] = split(here)
                cube[c, part, pl.ds(y, x_local, stride=y_local), :] = jnp.zeros_like(here)
            return carry

        lax.fori_loop(0, y_local, one, 0)

    def send_all(s, source, target, send_sem, recv_sem, own_sem):
        mine = pl.ds(pl.multiple_of(me * rows, rows), rows)
        pltpu.make_async_copy(source.at[s, mine, :], target.at[s, mine, :], own_sem.at[s]).start()

        def one(i, carry):
            t = (me + i) % count
            pltpu.make_async_remote_copy(
                src_ref=source.at[s, pl.ds(pl.multiple_of(t * rows, rows), rows), :],
                dst_ref=target.at[s, mine, :],
                send_sem=send_sem,
                recv_sem=recv_sem.at[s],
                device_id=place(t),
                device_id_type=MESH,
            ).start()
            return carry

        lax.fori_loop(1, count, one, 0)

    def receive_all(s, target, recv_sem, own_sem):
        own = target.at[s, pl.ds(0, rows), :]
        pltpu.make_async_copy(own, own, own_sem.at[s]).wait()
        others = target.at[s, pl.ds(0, (count - 1) * rows), :]
        pltpu.make_async_copy(others, others, recv_sem.at[s]).wait()

    def transform_lines(s):
        slot = s % slots
        both = stacked[pl.ds(pl.multiple_of(2 * slot * count, count), 2 * count), :]
        width = 4 * LANES

        def part(n, carry):
            where = pl.ds(pl.multiple_of(n * width, width), width)
            with_high = lax.dot_general(both, lines_high[where, :], NT, preferred_element_type=F32)
            with_low = lax.dot_general(
                both[:count], lines_low[where, :], NT, preferred_element_type=F32
            )
            value = with_high[:count] + with_high[count:] + with_low
            for q in range(4):
                send_there[s, pl.ds(n * 4 + q, count, stride=rows), :] = value[
                    :, q * LANES : (q + 1) * LANES
                ]
            return carry

        lax.fori_loop(0, cells // width, part, 0)

    for c in range(cols):
        column_wait(c)
        prepare(c)
        if c == 0:
            transform_lines(0)
            pl.semaphore_wait(barrier, count - 1)
            send_all(0, send_there, planes, there_sem, there_recv, own_there_sem)

        def forward(s, carry):
            transform_lines(s)
            send_all(s, send_there, planes, there_sem, there_recv, own_there_sem)
            return carry

        lax.fori_loop(1 if c == 0 else c * slots, (c + 1) * slots, forward, 0)

    for b in range(1, len(bases)):
        base_wait(b)
        for part in range(lane_parts):
            high, low = split(send_back[b, part * length : (part + 1) * length, :])
            lanes = slice(part * LANES, (part + 1) * LANES)
            bases_high[b - 1, :, lanes] = high
            bases_low[b - 1, :, lanes] = low
    eig_y_down = jnp.broadcast_to(eig_y[...], (LANES, length)).T
    for part in range(lane_parts):
        lanes = slice(part * LANES, (part + 1) * LANES)
        eig_sum[:, lanes] = eig_x[:, lanes] + eig_y_down

    first_half = lax.broadcasted_iota(jnp.int32, (1, LANES), 1) < x_local
    half = 2 * LANES

    def solve_plane(s):
        slot = s % slots
        shift = shift_table[shift_index[s // slots]]
        eig_z_here = eig_z[slot * count + me]
        block = pen_count * rows
        for h in range(lane_parts):
            a = planes[s, 2 * h * block : (2 * h + 1) * block, :]
            b = planes[s, (2 * h + 1) * block : (2 * h + 2) * block, :]
            low_y = jnp.where(first_half, a, pltpu.roll(b, x_local, 1))
            high_y = jnp.where(first_half, pltpu.roll(a, x_local, 1), b)
            low_y = low_y.reshape(pen_count, 1, rows, LANES)
            high_y = high_y.reshape(pen_count, 1, rows, LANES)
            both = jnp.concatenate([low_y, high_y], axis=1).reshape(length, LANES)
            lanes = slice(h * LANES, (h + 1) * LANES)
            first_high[:, lanes], first_low[:, lanes] = split(both)
        for n in range(length // half):
            lanes = slice(n * half, (n + 1) * half)
            value = product(
                (bases_high[0], bases_low[0]), (first_high[:, lanes], first_low[:, lanes]), NN
            )
            second_high[:, lanes], second_low[:, lanes] = split(value)
        scaling = jnp.sqrt(jnp.full((1, half), 2.0 * shift, F32))
        for n in range(length // half):
            lanes = slice(n * half, (n + 1) * half)
            value = product(
                (second_high[...], second_low[...]),
                (bases_high[1, lanes, :], bases_low[1, lanes, :]),
                NT,
            )
            value = scaling * value / (eig_sum[:, lanes] + eig_z_here + shift)
            first_high[:, lanes], first_low[:, lanes] = split(value)
        for n in range(length // half):
            lanes = slice(n * half, (n + 1) * half)
            value = product(
                (first_high[...], first_low[...]),
                (bases_high[2, lanes, :], bases_low[2, lanes, :]),
                NT,
            )
            second_high[:, lanes], second_low[:, lanes] = split(value)
        for n in range(length // half):
            lanes = slice(n * half, (n + 1) * half)
            value = product(
                (bases_high[3], bases_low[3]), (second_high[:, lanes], second_low[:, lanes]), NN
            )
            for i in range(2):
                h = 2 * n + i
                part = value[:, i * LANES : (i + 1) * LANES].reshape(pen_count, 2, rows, LANES)
                low_y = part[:, 0].reshape(block, LANES)
                high_y = part[:, 1].reshape(block, LANES)
                send_back[s, 2 * h * block : (2 * h + 1) * block, :] = jnp.where(
                    first_half, low_y, pltpu.roll(high_y, x_local, 1)
                )
                send_back[s, (2 * h + 1) * block : (2 * h + 2) * block, :] = jnp.where(
                    first_half, pltpu.roll(low_y, x_local, 1), high_y
                )

    def middle(s, carry):
        receive_all(s, planes, there_recv, own_there_sem)
        solve_plane(s)
        send_all(s, send_back, returned, back_sem, back_recv, own_back_sem)
        return carry

    lax.fori_loop(0, steps, middle, 0)

    def restore_lines(s):
        c, slot = s // slots, s % slots
        ks = pl.ds(pl.multiple_of(slot * count, count), count)
        right = (bases_high[4, :, ks], bases_low[4, :, ks])
        group = 4

        def part(n, carry):
            left = jnp.concatenate(
                [
                    returned[s, pl.ds(n * group + q, count, stride=rows), :].T
                    for q in range(group)
                ],
                axis=0,
            )
            value = product(split(left), right, NT)
            for q in range(group):
                for high in range(LANES // x_local):
                    start = q * LANES + high * x_local
                    y = high * rows + n * group + q
                    to = pl.ds(y, x_local, stride=y_local)
                    for p in range(lane_parts):
                        cube[c, p, to, :] = (
                            cube[c, p, to, :]
                            + value[start : start + x_local, p * LANES : (p + 1) * LANES]
                        )
            return carry

        lax.fori_loop(0, rows // group, part, 0)

    def backward(s, carry):
        receive_all(s, returned, back_recv, own_back_sem)
        restore_lines(s)
        return carry

    def column_store(c, part):
        lanes = pl.ds(part * LANES, LANES)
        return pltpu.make_async_copy(cube.at[c, part], solved.at[c, :, lanes], store_sem.at[c])

    for c in range(cols):
        lax.fori_loop(c * slots, (c + 1) * slots, backward, 0)
        for part in range(lane_parts):
            column_store(c, part).start()
    sent = pl.ds(0, (count - 1) * rows)
    for source, sem in ((send_there, there_sem), (send_back, back_sem)):
        whole = source.at[:, sent, :]
        pltpu.make_async_copy(whole, whole, sem).wait()
    for c in range(cols):
        pltpu.make_async_copy(cube.at[c], cube.at[c], store_sem.at[c]).wait()


def per_device(
    columns,
    basis_in_x,
    basis_in_y,
    basis_in_z,
    basis_out_x,
    basis_out_y,
    basis_out_z,
    eig_x,
    eig_y,
    eig_z,
    shift_table,
    shift_index,
):
    cols, x_local, y_local, length = columns.shape
    cells = x_local * y_local
    count = lax.axis_size("grp") * lax.axis_size("pen")
    slots = length // count
    steps = cols * slots
    smem = pl.BlockSpec(memory_space=pltpu.SMEM)
    vmem = pl.BlockSpec(memory_space=pltpu.VMEM)
    far = pl.BlockSpec(memory_space=pl.ANY)
    messages = pltpu.VMEM((steps, cells * count // LANES, LANES), F32)
    square = pltpu.VMEM((length, length), BF16)
    dma = pltpu.SemaphoreType.DMA
    solved = pl.pallas_call(
        solve_kernel,
        out_shape=jax.ShapeDtypeStruct((cols, cells, length), F32),
        in_specs=[smem, smem, smem, vmem, vmem] + [far] * 7,
        out_specs=far,
        scratch_shapes=[
            pltpu.VMEM((cols, length // LANES, cells, LANES), F32),
            pltpu.VMEM((cells, length), BF16),
            pltpu.VMEM((cells, length), BF16),
            messages,
            messages,
            messages,
            messages,
            pltpu.VMEM((2 * length, length), BF16),
            pltpu.VMEM((5, length, length), BF16),
            pltpu.VMEM((5, length, length), BF16),
            square,
            square,
            square,
            square,
            pltpu.VMEM((length, length), F32),
            dma((cols + 6,)),
            dma((cols,)),
            dma((steps,)),
            dma((steps,)),
            dma,
            dma,
            dma((steps,)),
            dma((steps,)),
        ],
        compiler_params=pltpu.CompilerParams(
            collective_id=0, has_side_effects=True, vmem_limit_bytes=67043328
        ),
        name="solve",
    )(
        shift_index,
        shift_table,
        eig_z,
        eig_x.reshape(1, length),
        eig_y.reshape(1, length),
        columns.reshape(cols, cells, length),
        basis_in_x,
        basis_in_y,
        basis_in_z,
        basis_out_x,
        basis_out_y,
        basis_out_z,
    )
    return solved.reshape(columns.shape)


def solution(mesh):
    in_specs = (P(None, "grp", "pen", None), P(), P(), P(), P(), P(), P(), P(), P(), P(), P(), P())
    out_specs = P(None, "grp", "pen", None)
    return jax.shard_map(
        per_device, mesh=mesh, in_specs=in_specs, out_specs=out_specs, check_vma=False
    )
```

```python
import jax
import jax.numpy as jnp
from jax import lax
from jax.experimental import pallas as pl
from jax.experimental.pallas import tpu as pltpu
from jax.sharding import PartitionSpec as P

MESH = pl.DeviceIdType.MESH
F32, BF16 = jnp.float32, jnp.bfloat16
NT = (((1,), (1,)), ((), ()))
NN = (((1,), (0,)), ((), ()))
LANES = 128


def split(value):
    high = value.astype(BF16)
    return high, (value - high.astype(F32)).astype(BF16)


def product(left, right, dims):
    def dot(a, b):
        return lax.dot_general(a, b, dims, preferred_element_type=F32)

    return dot(left[0], right[0]) + dot(left[1], right[0]) + dot(left[0], right[1])


def solve_kernel(
    shift_index,
    shift_table,
    eig_z,
    eig_x,
    eig_y,
    columns,
    basis_in_x,
    basis_in_y,
    basis_in_z,
    basis_out_x,
    basis_out_y,
    basis_out_z,
    solved,
    cube,
    lines_high,
    lines_low,
    send_there,
    planes,
    send_back,
    returned,
    stacked,
    bases_high,
    bases_low,
    first_high,
    first_low,
    second_high,
    second_low,
    eig_sum,
    load_sem,
    store_sem,
    own_there_sem,
    own_back_sem,
    there_sem,
    back_sem,
    there_recv,
    back_recv,
):
    grp_count, pen_count = lax.axis_size("grp"), lax.axis_size("pen")
    count = grp_count * pen_count
    cols, cells, length = columns.shape
    slots = length // count
    steps = cols * slots
    rows = cells // LANES
    y_local = length // pen_count
    x_local = length // grp_count
    me = lax.axis_index("grp") * pen_count + lax.axis_index("pen")

    def place(t):
        return {"grp": t // pen_count, "pen": t % pen_count}

    chip_x, chip_y = me // 2 % 4, me // pen_count % 4
    chip_z, core = me // 8 % 2 * 2 + me // 64, me % 2

    def flat(dx, dy, dz, dc):
        z = (chip_z + dz) % 4
        return (
            (z % 2) * 64 + (chip_y + dy) % 4 * 16 + (z // 2) * 8 + (chip_x + dx) % 4 * 2
            + (core + dc) % 2
        )

    bases = (basis_in_z, basis_in_x, basis_in_y, basis_out_y, basis_out_x, basis_out_z)
    lane_parts = length // LANES

    def base_part(b, part):
        return pltpu.make_async_copy(
            bases[b].at[:, pl.ds(part * LANES, LANES)],
            send_back.at[b, pl.ds(part * length, length), :],
            load_sem.at[cols + b],
        )

    def column_load(c):
        return pltpu.make_async_copy(columns.at[c], cube.at[c], load_sem.at[c])

    for part in range(lane_parts):
        base_part(0, part).start()
    for c in range(cols):
        column_load(c).start()
    for b in range(1, len(bases)):
        for part in range(lane_parts):
            base_part(b, part).start()

    barrier = pltpu.get_barrier_semaphore()

    def greet(i, carry):
        pl.semaphore_signal(
            barrier, inc=1, device_id=place((me + i) % count), device_id_type=MESH
        )
        return carry

    lax.fori_loop(1, count, greet, 0)

    def base_wait(b):
        whole = send_back.at[b]
        pltpu.make_async_copy(whole, whole, load_sem.at[cols + b]).wait()

    base_wait(0)
    for part in range(lane_parts):
        for slot in range(slots):
            start = part * length + slot * count
            high, low = split(send_back[0, start : start + count, :])
            lanes = slice(part * LANES, (part + 1) * LANES)
            stacked[2 * slot * count : (2 * slot + 1) * count, lanes] = high
            stacked[(2 * slot + 1) * count : (2 * slot + 2) * count, lanes] = low

    def cell_block(group, r):
        return pl.ds(pl.multiple_of((r * rows + group) * y_local, y_local), y_local)

    def prepare(c):
        def one(x, carry):
            group, r = x % rows, x // rows
            to = pl.ds(pl.multiple_of(group * LANES + r * y_local, y_local), y_local)
            lines_high[to, :], lines_low[to, :] = split(cube[c, cell_block(group, r), :])
            return carry

        lax.fori_loop(0, x_local, one, 0)

    def send_all(s, source, target, send_sem, recv_sem, own_sem):
        mine = pl.ds(pl.multiple_of(me * rows, rows), rows)
        pltpu.make_async_copy(source.at[s, mine, :], target.at[s, mine, :], own_sem.at[s]).start()

        def some(i, carry):
            for u in range(4):
                for v in range(4):

                    def one(t=flat(u, u + v, u + i % 4, i // 4)):
                        pltpu.make_async_remote_copy(
                            src_ref=source.at[s, pl.ds(pl.multiple_of(t * rows, rows), rows), :],
                            dst_ref=target.at[s, mine, :],
                            send_sem=send_sem,
                            recv_sem=recv_sem.at[s],
                            device_id=place(t),
                            device_id_type=MESH,
                        ).start()

                    if u == 0 and v == 0:
                        pl.when(i > 0)(one)
                    else:
                        one()
            return carry

        lax.fori_loop(0, 8, some, 0)

    def receive_all(s, target, recv_sem, own_sem):
        own = target.at[s, pl.ds(0, rows), :]
        pltpu.make_async_copy(own, own, own_sem.at[s]).wait()
        others = target.at[s, pl.ds(0, (count - 1) * rows), :]
        pltpu.make_async_copy(others, others, recv_sem.at[s]).wait()

    def transform_lines(s):
        slot = s % slots
        both = stacked[pl.ds(pl.multiple_of(2 * slot * count, count), 2 * count), :]
        width = 4 * LANES

        def part(n, carry):
            where = pl.ds(pl.multiple_of(n * width, width), width)
            with_high = lax.dot_general(both, lines_high[where, :], NT, preferred_element_type=F32)
            with_low = lax.dot_general(
                both[:count], lines_low[where, :], NT, preferred_element_type=F32
            )
            value = with_high[:count] + with_high[count:] + with_low
            for q in range(4):
                send_there[s, pl.ds(n * 4 + q, count, stride=rows), :] = value[
                    :, q * LANES : (q + 1) * LANES
                ]
            return carry

        lax.fori_loop(0, cells // width, part, 0)

    for c in range(cols):
        column_load(c).wait()
        prepare(c)
        if c == 0:
            transform_lines(0)
            pl.semaphore_wait(barrier, count - 1)
            send_all(0, send_there, planes, there_sem, there_recv, own_there_sem)

        def forward(s, carry):
            transform_lines(s)
            send_all(s, send_there, planes, there_sem, there_recv, own_there_sem)
            return carry

        lax.fori_loop(1 if c == 0 else c * slots, (c + 1) * slots, forward, 0)

    for b in range(1, len(bases)):
        base_wait(b)
        for part in range(lane_parts):
            high, low = split(send_back[b, part * length : (part + 1) * length, :])
            lanes = slice(part * LANES, (part + 1) * LANES)
            bases_high[b - 1, :, lanes] = high
            bases_low[b - 1, :, lanes] = low
    eig_x_down = jnp.broadcast_to(eig_x[...], (LANES, length)).T
    for part in range(lane_parts):
        lanes = slice(part * LANES, (part + 1) * LANES)
        eig_sum[:, lanes] = eig_x_down + eig_y[:, lanes]

    lane = lax.broadcasted_iota(jnp.int32, (1, LANES), 1)
    first_half = lane < 2 * y_local
    even_part = lane % (2 * y_local) < y_local

    def exchange_parts(parts):
        def swap(a, b, keep, shift):
            return (
                jnp.where(keep, a, pltpu.roll(b, shift, 1)),
                jnp.where(keep, pltpu.roll(a, LANES - shift, 1), b),
            )

        a0, a1, a2, a3 = (parts[rows * j : rows * (j + 1)] for j in range(4))
        b0, b2 = swap(a0, a2, first_half, 2 * y_local)
        b1, b3 = swap(a1, a3, first_half, 2 * y_local)
        return jnp.concatenate(
            [*swap(b0, b1, even_part, y_local), *swap(b2, b3, even_part, y_local)], axis=0
        )

    def clear(i, carry):
        here = pl.ds(pl.multiple_of(i * y_local, y_local), y_local)
        for c in range(cols):
            cube[c, here, :] = jnp.zeros((y_local, length), F32)
        return carry

    lax.fori_loop(0, x_local, clear, 0)

    half = 2 * LANES

    def solve_plane(s):
        slot = s % slots
        shift = shift_table[shift_index[s // slots]]
        eig_z_here = eig_z[slot * count + me]
        for g in range(grp_count):
            for q in range(lane_parts):
                start = (g * pen_count + 4 * q) * rows
                block = exchange_parts(planes[s, start : start + 4 * rows, :])
                here, lanes = slice(g * x_local, (g + 1) * x_local), slice(q * LANES, (q + 1) * LANES)
                first_high[here, lanes], first_low[here, lanes] = split(block)
        for n in range(length // half):
            lanes = slice(n * half, (n + 1) * half)
            value = product(
                (bases_high[0], bases_low[0]), (first_high[:, lanes], first_low[:, lanes]), NN
            )
            second_high[:, lanes], second_low[:, lanes] = split(value)
        scaling = jnp.sqrt(jnp.full((1, half), 2.0 * shift, F32))
        for n in range(length // half):
            lanes = slice(n * half, (n + 1) * half)
            value = product(
                (second_high[...], second_low[...]),
                (bases_high[1, lanes, :], bases_low[1, lanes, :]),
                NT,
            )
            value = scaling * value / (eig_sum[:, lanes] + eig_z_here + shift)
            first_high[:, lanes], first_low[:, lanes] = split(value)
        for n in range(length // half):
            lanes = slice(n * half, (n + 1) * half)
            value = product(
                (first_high[...], first_low[...]),
                (bases_high[2, lanes, :], bases_low[2, lanes, :]),
                NT,
            )
            second_high[:, lanes], second_low[:, lanes] = split(value)
        for n in range(length // half):
            lanes = slice(n * half, (n + 1) * half)
            value = product(
                (bases_high[3], bases_low[3]), (second_high[:, lanes], second_low[:, lanes]), NN
            )
            for i in range(2):
                for g in range(grp_count):
                    start = (g * pen_count + 4 * (2 * n + i)) * rows
                    send_back[s, start : start + 4 * rows, :] = exchange_parts(
                        value[g * x_local : (g + 1) * x_local, i * LANES : (i + 1) * LANES]
                    )

    def middle(s, carry):
        receive_all(s, planes, there_recv, own_there_sem)
        solve_plane(s)
        send_all(s, send_back, returned, back_sem, back_recv, own_back_sem)
        return carry

    lax.fori_loop(0, steps, middle, 0)

    def restore_lines(s):
        c, slot = s // slots, s % slots
        ks = pl.ds(pl.multiple_of(slot * count, count), count)
        right = (bases_high[4, :, ks], bases_low[4, :, ks])
        group = 4

        def part(n, carry):
            left = jnp.concatenate(
                [
                    returned[s, pl.ds(n * group + q, count, stride=rows), :].T
                    for q in range(group)
                ],
                axis=0,
            )
            value = product(split(left), right, NT)
            for q in range(group):
                for r in range(LANES // y_local):
                    start = q * LANES + r * y_local
                    here = cell_block(n * group + q, r)
                    cube[c, here, :] = cube[c, here, :] + value[start : start + y_local]
            return carry

        lax.fori_loop(0, rows // group, part, 0)

    def backward(s, carry):
        receive_all(s, returned, back_recv, own_back_sem)
        restore_lines(s)
        return carry

    def column_store(c):
        return pltpu.make_async_copy(cube.at[c], solved.at[c], store_sem.at[c])

    for c in range(cols):
        lax.fori_loop(c * slots, (c + 1) * slots, backward, 0)
        column_store(c).start()
    sent = pl.ds(0, (count - 1) * rows)
    for source, sem in ((send_there, there_sem), (send_back, back_sem)):
        whole = source.at[:, sent, :]
        pltpu.make_async_copy(whole, whole, sem).wait()
    for c in range(cols):
        column_store(c).wait()


def per_device(
    columns,
    basis_in_x,
    basis_in_y,
    basis_in_z,
    basis_out_x,
    basis_out_y,
    basis_out_z,
    eig_x,
    eig_y,
    eig_z,
    shift_table,
    shift_index,
):
    cols, x_local, y_local, length = columns.shape
    cells = x_local * y_local
    count = lax.axis_size("grp") * lax.axis_size("pen")
    slots = length // count
    steps = cols * slots
    smem = pl.BlockSpec(memory_space=pltpu.SMEM)
    vmem = pl.BlockSpec(memory_space=pltpu.VMEM)
    far = pl.BlockSpec(memory_space=pl.ANY)
    messages = pltpu.VMEM((steps, cells * count // LANES, LANES), F32)
    square = pltpu.VMEM((length, length), BF16)
    dma = pltpu.SemaphoreType.DMA
    solved = pl.pallas_call(
        solve_kernel,
        out_shape=jax.ShapeDtypeStruct((cols, cells, length), F32),
        in_specs=[smem, smem, smem, vmem, vmem] + [far] * 7,
        out_specs=far,
        scratch_shapes=[
            pltpu.VMEM((cols, cells, length), F32),
            pltpu.VMEM((cells, length), BF16),
            pltpu.VMEM((cells, length), BF16),
            messages,
            messages,
            messages,
            messages,
            pltpu.VMEM((2 * length, length), BF16),
            pltpu.VMEM((5, length, length), BF16),
            pltpu.VMEM((5, length, length), BF16),
            square,
            square,
            square,
            square,
            pltpu.VMEM((length, length), F32),
            dma((cols + 6,)),
            dma((cols,)),
            dma((steps,)),
            dma((steps,)),
            dma,
            dma,
            dma((steps,)),
            dma((steps,)),
        ],
        compiler_params=pltpu.CompilerParams(
            collective_id=0, has_side_effects=True, vmem_limit_bytes=67043328
        ),
        name="solve",
    )(
        shift_index,
        shift_table,
        eig_z,
        eig_x.reshape(1, length),
        eig_y.reshape(1, length),
        columns.reshape(cols, cells, length),
        basis_in_x,
        basis_in_y,
        basis_in_z,
        basis_out_x,
        basis_out_y,
        basis_out_z,
    )
    return solved.reshape(columns.shape)


def solution(mesh):
    in_specs = (P(None, "grp", "pen", None), P(), P(), P(), P(), P(), P(), P(), P(), P(), P(), P())
    out_specs = P(None, "grp", "pen", None)
    return jax.shard_map(
        per_device, mesh=mesh, in_specs=in_specs, out_specs=out_specs, check_vma=False
    )
```

```python
import jax
import jax.numpy as jnp
from jax import lax
from jax.experimental import pallas as pl
from jax.experimental.pallas import tpu as pltpu
from jax.sharding import PartitionSpec as P

MESH = pl.DeviceIdType.MESH
F32, BF16 = jnp.float32, jnp.bfloat16
NT = (((1,), (1,)), ((), ()))
NN = (((1,), (0,)), ((), ()))
LANES = 128


def split(value):
    high = value.astype(BF16)
    return high, (value - high.astype(F32)).astype(BF16)


def product(left, right, dims):
    def dot(a, b):
        return lax.dot_general(a, b, dims, preferred_element_type=F32)

    return dot(left[0], right[0]) + dot(left[1], right[0]) + dot(left[0], right[1])


def solve_kernel(
    shift_index,
    shift_table,
    eig_z,
    eig_x,
    eig_y,
    columns,
    basis_in_x,
    basis_in_y,
    basis_in_z,
    basis_out_x,
    basis_out_y,
    basis_out_z,
    cube,
    lines_high,
    lines_low,
    send_there,
    planes,
    send_back,
    returned,
    stacked,
    bases_high,
    bases_low,
    first_high,
    first_low,
    second_high,
    second_low,
    eig_sum,
    load_sem,
    own_there_sem,
    own_back_sem,
    there_sem,
    back_sem,
    there_recv,
    back_recv,
):
    grp_count, pen_count = lax.axis_size("grp"), lax.axis_size("pen")
    count = grp_count * pen_count
    cols, cells, length = columns.shape
    slots = length // count
    steps = cols * slots
    rows = cells // LANES
    y_local = length // pen_count
    x_local = length // grp_count
    me = lax.axis_index("grp") * pen_count + lax.axis_index("pen")

    def place(t):
        return {"grp": t // pen_count, "pen": t % pen_count}

    chip_x, chip_y = me // 2 % 4, me // pen_count % 4
    chip_z, core = me // 8 % 2 * 2 + me // 64, me % 2

    def flat(dx, dy, dz, dc):
        z = (chip_z + dz) % 4
        return (
            (z % 2) * 64 + (chip_y + dy) % 4 * 16 + (z // 2) * 8 + (chip_x + dx) % 4 * 2
            + (core + dc) % 2
        )

    bases = (basis_in_z, basis_in_x, basis_in_y, basis_out_y, basis_out_x, basis_out_z)
    lane_parts = length // LANES

    def base_part(b, part):
        return pltpu.make_async_copy(
            bases[b].at[:, pl.ds(part * LANES, LANES)],
            send_back.at[b, pl.ds(part * length, length), :],
            load_sem.at[cols + b],
        )

    def column_load(c):
        return pltpu.make_async_copy(columns.at[c], cube.at[c], load_sem.at[c])

    for part in range(lane_parts):
        base_part(0, part).start()
    for c in range(cols):
        column_load(c).start()
    for b in range(1, len(bases)):
        for part in range(lane_parts):
            base_part(b, part).start()

    barrier = pltpu.get_barrier_semaphore()

    def greet(i, carry):
        pl.semaphore_signal(
            barrier, inc=1, device_id=place((me + i) % count), device_id_type=MESH
        )
        return carry

    lax.fori_loop(1, count, greet, 0)

    def base_wait(b):
        whole = send_back.at[b]
        pltpu.make_async_copy(whole, whole, load_sem.at[cols + b]).wait()

    base_wait(0)
    for part in range(lane_parts):
        for slot in range(slots):
            start = part * length + slot * count
            high, low = split(send_back[0, start : start + count, :])
            lanes = slice(part * LANES, (part + 1) * LANES)
            stacked[2 * slot * count : (2 * slot + 1) * count, lanes] = high
            stacked[(2 * slot + 1) * count : (2 * slot + 2) * count, lanes] = low

    def cell_block(group, r):
        return pl.ds(pl.multiple_of((r * rows + group) * y_local, y_local), y_local)

    def prepare(c):
        def one(x, carry):
            group, r = x % rows, x // rows
            to = pl.ds(pl.multiple_of(group * LANES + r * y_local, y_local), y_local)
            lines_high[to, :], lines_low[to, :] = split(cube[c, cell_block(group, r), :])
            return carry

        lax.fori_loop(0, x_local, one, 0)

    def send_all(s, source, target, send_sem, recv_sem, own_sem):
        mine = pl.ds(pl.multiple_of(me * rows, rows), rows)
        pltpu.make_async_copy(source.at[s, mine, :], target.at[s, mine, :], own_sem.at[s]).start()

        def some(i, carry):
            for u in range(4):
                for v in range(4):

                    def one(t=flat(u, u + v, u + i % 4, i // 4)):
                        pltpu.make_async_remote_copy(
                            src_ref=source.at[s, pl.ds(pl.multiple_of(t * rows, rows), rows), :],
                            dst_ref=target.at[s, mine, :],
                            send_sem=send_sem,
                            recv_sem=recv_sem.at[s],
                            device_id=place(t),
                            device_id_type=MESH,
                        ).start()

                    if u == 0 and v == 0:
                        pl.when(i > 0)(one)
                    else:
                        one()
            return carry

        lax.fori_loop(0, 8, some, 0)

    def receive_all(s, target, recv_sem, own_sem):
        own = target.at[s, pl.ds(0, rows), :]
        pltpu.make_async_copy(own, own, own_sem.at[s]).wait()
        others = target.at[s, pl.ds(0, (count - 1) * rows), :]
        pltpu.make_async_copy(others, others, recv_sem.at[s]).wait()

    def transform_lines(s):
        slot = s % slots
        both = stacked[pl.ds(pl.multiple_of(2 * slot * count, count), 2 * count), :]
        width = 4 * LANES

        def part(n, carry):
            where = pl.ds(pl.multiple_of(n * width, width), width)
            with_high = lax.dot_general(both, lines_high[where, :], NT, preferred_element_type=F32)
            with_low = lax.dot_general(
                both[:count], lines_low[where, :], NT, preferred_element_type=F32
            )
            value = with_high[:count] + with_high[count:] + with_low
            for q in range(4):
                send_there[s, pl.ds(n * 4 + q, count, stride=rows), :] = value[
                    :, q * LANES : (q + 1) * LANES
                ]
            return carry

        lax.fori_loop(0, cells // width, part, 0)

    for c in range(cols):
        column_load(c).wait()
        prepare(c)
        if c == 0:
            transform_lines(0)
            pl.semaphore_wait(barrier, count - 1)
            send_all(0, send_there, planes, there_sem, there_recv, own_there_sem)

        def forward(s, carry):
            transform_lines(s)
            send_all(s, send_there, planes, there_sem, there_recv, own_there_sem)
            return carry

        lax.fori_loop(1 if c == 0 else c * slots, (c + 1) * slots, forward, 0)

    for b in range(1, len(bases)):
        base_wait(b)
        for part in range(lane_parts):
            high, low = split(send_back[b, part * length : (part + 1) * length, :])
            lanes = slice(part * LANES, (part + 1) * LANES)
            bases_high[b - 1, :, lanes] = high
            bases_low[b - 1, :, lanes] = low
    eig_x_down = jnp.broadcast_to(eig_x[...], (LANES, length)).T
    for part in range(lane_parts):
        lanes = slice(part * LANES, (part + 1) * LANES)
        eig_sum[:, lanes] = eig_x_down + eig_y[:, lanes]

    lane = lax.broadcasted_iota(jnp.int32, (1, LANES), 1)
    first_half = lane < 2 * y_local
    even_part = lane % (2 * y_local) < y_local

    def exchange_parts(parts):
        def swap(a, b, keep, shift):
            return (
                jnp.where(keep, a, pltpu.roll(b, shift, 1)),
                jnp.where(keep, pltpu.roll(a, LANES - shift, 1), b),
            )

        a0, a1, a2, a3 = (parts[rows * j : rows * (j + 1)] for j in range(4))
        b0, b2 = swap(a0, a2, first_half, 2 * y_local)
        b1, b3 = swap(a1, a3, first_half, 2 * y_local)
        return jnp.concatenate(
            [*swap(b0, b1, even_part, y_local), *swap(b2, b3, even_part, y_local)], axis=0
        )

    def clear(i, carry):
        here = pl.ds(pl.multiple_of(i * y_local, y_local), y_local)
        for c in range(cols):
            cube[c, here, :] = jnp.zeros((y_local, length), F32)
        return carry

    lax.fori_loop(0, x_local, clear, 0)

    half = 2 * LANES

    def solve_plane(s):
        slot = s % slots
        shift = shift_table[shift_index[s // slots]]
        eig_z_here = eig_z[slot * count + me]
        for g in range(grp_count):
            for q in range(lane_parts):
                start = (g * pen_count + 4 * q) * rows
                block = exchange_parts(planes[s, start : start + 4 * rows, :])
                here, lanes = slice(g * x_local, (g + 1) * x_local), slice(q * LANES, (q + 1) * LANES)
                first_high[here, lanes], first_low[here, lanes] = split(block)
        for n in range(length // half):
            lanes = slice(n * half, (n + 1) * half)
            value = product(
                (bases_high[0], bases_low[0]), (first_high[:, lanes], first_low[:, lanes]), NN
            )
            second_high[:, lanes], second_low[:, lanes] = split(value)
        scaling = jnp.sqrt(jnp.full((1, half), 2.0 * shift, F32))
        for n in range(length // half):
            lanes = slice(n * half, (n + 1) * half)
            value = product(
                (second_high[...], second_low[...]),
                (bases_high[1, lanes, :], bases_low[1, lanes, :]),
                NT,
            )
            value = scaling * value / (eig_sum[:, lanes] + eig_z_here + shift)
            first_high[:, lanes], first_low[:, lanes] = split(value)
        for n in range(length // half):
            lanes = slice(n * half, (n + 1) * half)
            value = product(
                (first_high[...], first_low[...]),
                (bases_high[2, lanes, :], bases_low[2, lanes, :]),
                NT,
            )
            second_high[:, lanes], second_low[:, lanes] = split(value)
        for n in range(length // half):
            lanes = slice(n * half, (n + 1) * half)
            value = product(
                (bases_high[3], bases_low[3]), (second_high[:, lanes], second_low[:, lanes]), NN
            )
            for i in range(2):
                for g in range(grp_count):
                    start = (g * pen_count + 4 * (2 * n + i)) * rows
                    send_back[s, start : start + 4 * rows, :] = exchange_parts(
                        value[g * x_local : (g + 1) * x_local, i * LANES : (i + 1) * LANES]
                    )

    def middle(s, carry):
        receive_all(s, planes, there_recv, own_there_sem)
        solve_plane(s)
        send_all(s, send_back, returned, back_sem, back_recv, own_back_sem)
        return carry

    lax.fori_loop(0, steps, middle, 0)

    def restore_lines(s):
        c, slot = s // slots, s % slots
        ks = pl.ds(pl.multiple_of(slot * count, count), count)
        right = (bases_high[4, :, ks], bases_low[4, :, ks])
        group = 4

        def part(n, carry):
            left = jnp.concatenate(
                [
                    returned[s, pl.ds(n * group + q, count, stride=rows), :].T
                    for q in range(group)
                ],
                axis=0,
            )
            value = product(split(left), right, NT)
            for q in range(group):
                for r in range(LANES // y_local):
                    start = q * LANES + r * y_local
                    here = cell_block(n * group + q, r)
                    cube[c, here, :] = cube[c, here, :] + value[start : start + y_local]
            return carry

        lax.fori_loop(0, rows // group, part, 0)

    def backward(s, carry):
        receive_all(s, returned, back_recv, own_back_sem)
        restore_lines(s)
        return carry

    for c in range(cols):
        lax.fori_loop(c * slots, (c + 1) * slots, backward, 0)
    sent = pl.ds(0, (count - 1) * rows)
    for source, sem in ((send_there, there_sem), (send_back, back_sem)):
        whole = source.at[:, sent, :]
        pltpu.make_async_copy(whole, whole, sem).wait()


def per_device(
    columns,
    basis_in_x,
    basis_in_y,
    basis_in_z,
    basis_out_x,
    basis_out_y,
    basis_out_z,
    eig_x,
    eig_y,
    eig_z,
    shift_table,
    shift_index,
):
    cols, x_local, y_local, length = columns.shape
    cells = x_local * y_local
    count = lax.axis_size("grp") * lax.axis_size("pen")
    slots = length // count
    steps = cols * slots
    smem = pl.BlockSpec(memory_space=pltpu.SMEM)
    vmem = pl.BlockSpec(memory_space=pltpu.VMEM)
    far = pl.BlockSpec(memory_space=pl.ANY)
    messages = pltpu.VMEM((steps, cells * count // LANES, LANES), F32)
    square = pltpu.VMEM((length, length), BF16)
    dma = pltpu.SemaphoreType.DMA
    solved = pl.pallas_call(
        solve_kernel,
        out_shape=pltpu.VMEM((cols, cells, length), F32),
        in_specs=[smem, smem, smem, vmem, vmem] + [far] * 7,
        out_specs=vmem,
        scratch_shapes=[
            pltpu.VMEM((cells, length), BF16),
            pltpu.VMEM((cells, length), BF16),
            messages,
            messages,
            messages,
            messages,
            pltpu.VMEM((2 * length, length), BF16),
            pltpu.VMEM((5, length, length), BF16),
            pltpu.VMEM((5, length, length), BF16),
            square,
            square,
            square,
            square,
            pltpu.VMEM((length, length), F32),
            dma((cols + 6,)),
            dma((steps,)),
            dma((steps,)),
            dma,
            dma,
            dma((steps,)),
            dma((steps,)),
        ],
        compiler_params=pltpu.CompilerParams(
            collective_id=0, has_side_effects=True, vmem_limit_bytes=54 * 2**20
        ),
        name="solve",
    )(
        shift_index,
        shift_table,
        eig_z,
        eig_x.reshape(1, length),
        eig_y.reshape(1, length),
        columns.reshape(cols, cells, length),
        basis_in_x,
        basis_in_y,
        basis_in_z,
        basis_out_x,
        basis_out_y,
        basis_out_z,
    )
    return solved.reshape(columns.shape)


def solution(mesh):
    in_specs = (P(None, "grp", "pen", None), P(), P(), P(), P(), P(), P(), P(), P(), P(), P(), P())
    out_specs = P(None, "grp", "pen", None)
    return jax.shard_map(
        per_device, mesh=mesh, in_specs=in_specs, out_specs=out_specs, check_vma=False
    )
```

```python
import jax
import jax.numpy as jnp
from jax import lax
from jax.experimental import pallas as pl
from jax.experimental.pallas import tpu as pltpu
from jax.sharding import PartitionSpec as P

MESH = pl.DeviceIdType.MESH
F32, BF16 = jnp.float32, jnp.bfloat16
NT = (((1,), (1,)), ((), ()))
NN = (((1,), (0,)), ((), ()))
LANES = 128


def split(value):
    high = value.astype(BF16)
    return high, (value - high.astype(F32)).astype(BF16)


def product(left, right, dims):
    def dot(a, b):
        return lax.dot_general(a, b, dims, preferred_element_type=F32)

    return dot(left[0], right[0]) + dot(left[1], right[0]) + dot(left[0], right[1])


def solve_kernel(
    shift_index,
    shift_table,
    eig_z,
    eig_x,
    eig_y,
    columns,
    basis_in_x,
    basis_in_y,
    basis_in_z,
    basis_out_x,
    basis_out_y,
    basis_out_z,
    cube,
    lines_high,
    lines_low,
    send_there,
    planes,
    send_back,
    returned,
    stacked,
    bases_high,
    bases_low,
    first_high,
    first_low,
    second_high,
    second_low,
    eig_sum,
    load_sem,
    own_there_sem,
    own_back_sem,
    there_sem,
    back_sem,
    there_recv,
    back_recv,
):
    grp_count, pen_count = lax.axis_size("grp"), lax.axis_size("pen")
    count = grp_count * pen_count
    cols, cells, length = columns.shape
    slots = length // count
    steps = cols * slots
    rows = cells // LANES
    y_local = length // pen_count
    x_local = length // grp_count
    me = lax.axis_index("grp") * pen_count + lax.axis_index("pen")

    def place(t):
        return {"grp": t // pen_count, "pen": t % pen_count}

    chip_x, chip_y = me // 2 % 4, me // pen_count % 4
    chip_z, core = me // 8 % 2 * 2 + me // 64, me % 2
    sign = 1 - 2 * core

    def flat(dx, dy, dz, dc):
        z = (chip_z + 8 + sign * dz) % 4
        return (
            (z % 2) * 64 + (chip_y + 8 + sign * dy) % 4 * 16 + (z // 2) * 8 + (chip_x + 8 + sign * dx) % 4 * 2
            + (core + dc) % 2
        )

    bases = (basis_in_z, basis_in_x, basis_in_y, basis_out_y, basis_out_x, basis_out_z)
    lane_parts = length // LANES

    def base_part(b, part):
        return pltpu.make_async_copy(
            bases[b].at[:, pl.ds(part * LANES, LANES)],
            send_back.at[b, pl.ds(part * length, length), :],
            load_sem.at[cols + b],
        )

    def column_load(c):
        return pltpu.make_async_copy(columns.at[c], cube.at[c], load_sem.at[c])

    for part in range(lane_parts):
        base_part(0, part).start()
    for c in range(cols):
        column_load(c).start()
    for b in range(1, len(bases)):
        for part in range(lane_parts):
            base_part(b, part).start()

    barrier = pltpu.get_barrier_semaphore()

    def greet(i, carry):
        pl.semaphore_signal(
            barrier, inc=1, device_id=place((me + i) % count), device_id_type=MESH
        )
        return carry

    lax.fori_loop(1, count, greet, 0)

    def base_wait(b):
        whole = send_back.at[b]
        pltpu.make_async_copy(whole, whole, load_sem.at[cols + b]).wait()

    base_wait(0)
    for part in range(lane_parts):
        for slot in range(slots):
            start = part * length + slot * count
            high, low = split(send_back[0, start : start + count, :])
            lanes = slice(part * LANES, (part + 1) * LANES)
            stacked[2 * slot * count : (2 * slot + 1) * count, lanes] = high
            stacked[(2 * slot + 1) * count : (2 * slot + 2) * count, lanes] = low

    def cell_block(group, r):
        return pl.ds(pl.multiple_of((r * rows + group) * y_local, y_local), y_local)

    def prepare(c):
        def one(x, carry):
            group, r = x % rows, x // rows
            to = pl.ds(pl.multiple_of(group * LANES + r * y_local, y_local), y_local)
            lines_high[to, :], lines_low[to, :] = split(cube[c, cell_block(group, r), :])
            return carry

        lax.fori_loop(0, x_local, one, 0)

    def send_all(s, source, target, send_sem, recv_sem, own_sem):
        mine = pl.ds(pl.multiple_of(me * rows, rows), rows)
        pltpu.make_async_copy(source.at[s, mine, :], target.at[s, mine, :], own_sem.at[s]).start()

        def some(i, carry):
            for u in range(4):
                for v in range(4):

                    def one(t=flat(u, u + v, u + i % 4, i // 4)):
                        pltpu.make_async_remote_copy(
                            src_ref=source.at[s, pl.ds(pl.multiple_of(t * rows, rows), rows), :],
                            dst_ref=target.at[s, mine, :],
                            send_sem=send_sem,
                            recv_sem=recv_sem.at[s],
                            device_id=place(t),
                            device_id_type=MESH,
                        ).start()

                    if u == 0 and v == 0:
                        pl.when(i > 0)(one)
                    else:
                        one()
            return carry

        lax.fori_loop(0, 8, some, 0)

    def receive_all(s, target, recv_sem, own_sem):
        own = target.at[s, pl.ds(0, rows), :]
        pltpu.make_async_copy(own, own, own_sem.at[s]).wait()
        others = target.at[s, pl.ds(0, (count - 1) * rows), :]
        pltpu.make_async_copy(others, others, recv_sem.at[s]).wait()

    def transform_lines(s):
        slot = s % slots
        both = stacked[pl.ds(pl.multiple_of(2 * slot * count, count), 2 * count), :]
        width = 4 * LANES

        def part(n, carry):
            where = pl.ds(pl.multiple_of(n * width, width), width)
            with_high = lax.dot_general(both, lines_high[where, :], NT, preferred_element_type=F32)
            with_low = lax.dot_general(
                both[:count], lines_low[where, :], NT, preferred_element_type=F32
            )
            value = with_high[:count] + with_high[count:] + with_low
            for q in range(4):
                send_there[s, pl.ds(n * 4 + q, count, stride=rows), :] = value[
                    :, q * LANES : (q + 1) * LANES
                ]
            return carry

        lax.fori_loop(0, cells // width, part, 0)

    for c in range(cols):
        column_load(c).wait()
        prepare(c)
        if c == 0:
            transform_lines(0)
            pl.semaphore_wait(barrier, count - 1)
            send_all(0, send_there, planes, there_sem, there_recv, own_there_sem)

        def forward(s, carry):
            transform_lines(s)
            send_all(s, send_there, planes, there_sem, there_recv, own_there_sem)
            return carry

        lax.fori_loop(1 if c == 0 else c * slots, (c + 1) * slots, forward, 0)

    for b in range(1, len(bases)):
        base_wait(b)
        for part in range(lane_parts):
            high, low = split(send_back[b, part * length : (part + 1) * length, :])
            lanes = slice(part * LANES, (part + 1) * LANES)
            bases_high[b - 1, :, lanes] = high
            bases_low[b - 1, :, lanes] = low
    eig_x_down = jnp.broadcast_to(eig_x[...], (LANES, length)).T
    for part in range(lane_parts):
        lanes = slice(part * LANES, (part + 1) * LANES)
        eig_sum[:, lanes] = eig_x_down + eig_y[:, lanes]

    lane = lax.broadcasted_iota(jnp.int32, (1, LANES), 1)
    first_half = lane < 2 * y_local
    even_part = lane % (2 * y_local) < y_local

    def exchange_parts(parts):
        def swap(a, b, keep, shift):
            return (
                jnp.where(keep, a, pltpu.roll(b, shift, 1)),
                jnp.where(keep, pltpu.roll(a, LANES - shift, 1), b),
            )

        a0, a1, a2, a3 = (parts[rows * j : rows * (j + 1)] for j in range(4))
        b0, b2 = swap(a0, a2, first_half, 2 * y_local)
        b1, b3 = swap(a1, a3, first_half, 2 * y_local)
        return jnp.concatenate(
            [*swap(b0, b1, even_part, y_local), *swap(b2, b3, even_part, y_local)], axis=0
        )

    def clear(i, carry):
        here = pl.ds(pl.multiple_of(i * y_local, y_local), y_local)
        for c in range(cols):
            cube[c, here, :] = jnp.zeros((y_local, length), F32)
        return carry

    lax.fori_loop(0, x_local, clear, 0)

    half = 2 * LANES

    def solve_plane(s):
        slot = s % slots
        shift = shift_table[shift_index[s // slots]]
        eig_z_here = eig_z[slot * count + me]
        for g in range(grp_count):
            for q in range(lane_parts):
                start = (g * pen_count + 4 * q) * rows
                block = exchange_parts(planes[s, start : start + 4 * rows, :])
                here, lanes = slice(g * x_local, (g + 1) * x_local), slice(q * LANES, (q + 1) * LANES)
                first_high[here, lanes], first_low[here, lanes] = split(block)
        for n in range(length // half):
            lanes = slice(n * half, (n + 1) * half)
            value = product(
                (bases_high[0], bases_low[0]), (first_high[:, lanes], first_low[:, lanes]), NN
            )
            second_high[:, lanes], second_low[:, lanes] = split(value)
        scaling = jnp.sqrt(jnp.full((1, half), 2.0 * shift, F32))
        for n in range(length // half):
            lanes = slice(n * half, (n + 1) * half)
            value = product(
                (second_high[...], second_low[...]),
                (bases_high[1, lanes, :], bases_low[1, lanes, :]),
                NT,
            )
            value = scaling * value / (eig_sum[:, lanes] + eig_z_here + shift)
            first_high[:, lanes], first_low[:, lanes] = split(value)
        for n in range(length // half):
            lanes = slice(n * half, (n + 1) * half)
            value = product(
                (first_high[...], first_low[...]),
                (bases_high[2, lanes, :], bases_low[2, lanes, :]),
                NT,
            )
            second_high[:, lanes], second_low[:, lanes] = split(value)
        for n in range(length // half):
            lanes = slice(n * half, (n + 1) * half)
            value = product(
                (bases_high[3], bases_low[3]), (second_high[:, lanes], second_low[:, lanes]), NN
            )
            for i in range(2):
                for g in range(grp_count):
                    start = (g * pen_count + 4 * (2 * n + i)) * rows
                    send_back[s, start : start + 4 * rows, :] = exchange_parts(
                        value[g * x_local : (g + 1) * x_local, i * LANES : (i + 1) * LANES]
                    )

    def middle(s, carry):
        receive_all(s, planes, there_recv, own_there_sem)
        solve_plane(s)
        send_all(s, send_back, returned, back_sem, back_recv, own_back_sem)
        return carry

    lax.fori_loop(0, steps, middle, 0)

    def restore_lines(s):
        c, slot = s // slots, s % slots
        ks = pl.ds(pl.multiple_of(slot * count, count), count)
        right = (bases_high[4, :, ks], bases_low[4, :, ks])
        group = 4

        def part(n, carry):
            left = jnp.concatenate(
                [
                    returned[s, pl.ds(n * group + q, count, stride=rows), :].T
                    for q in range(group)
                ],
                axis=0,
            )
            value = product(split(left), right, NT)
            for q in range(group):
                for r in range(LANES // y_local):
                    start = q * LANES + r * y_local
                    here = cell_block(n * group + q, r)
                    cube[c, here, :] = cube[c, here, :] + value[start : start + y_local]
            return carry

        lax.fori_loop(0, rows // group, part, 0)

    def backward(s, carry):
        receive_all(s, returned, back_recv, own_back_sem)
        restore_lines(s)
        return carry

    for c in range(cols):
        lax.fori_loop(c * slots, (c + 1) * slots, backward, 0)
    sent = pl.ds(0, (count - 1) * rows)
    for source, sem in ((send_there, there_sem), (send_back, back_sem)):
        whole = source.at[:, sent, :]
        pltpu.make_async_copy(whole, whole, sem).wait()


def per_device(
    columns,
    basis_in_x,
    basis_in_y,
    basis_in_z,
    basis_out_x,
    basis_out_y,
    basis_out_z,
    eig_x,
    eig_y,
    eig_z,
    shift_table,
    shift_index,
):
    cols, x_local, y_local, length = columns.shape
    cells = x_local * y_local
    count = lax.axis_size("grp") * lax.axis_size("pen")
    slots = length // count
    steps = cols * slots
    smem = pl.BlockSpec(memory_space=pltpu.SMEM)
    vmem = pl.BlockSpec(memory_space=pltpu.VMEM)
    far = pl.BlockSpec(memory_space=pl.ANY)
    messages = pltpu.VMEM((steps, cells * count // LANES, LANES), F32)
    square = pltpu.VMEM((length, length), BF16)
    dma = pltpu.SemaphoreType.DMA
    solved = pl.pallas_call(
        solve_kernel,
        out_shape=pltpu.VMEM((cols, cells, length), F32),
        in_specs=[smem, smem, smem, vmem, vmem] + [far] * 7,
        out_specs=vmem,
        scratch_shapes=[
            pltpu.VMEM((cells, length), BF16),
            pltpu.VMEM((cells, length), BF16),
            messages,
            messages,
            messages,
            messages,
            pltpu.VMEM((2 * length, length), BF16),
            pltpu.VMEM((5, length, length), BF16),
            pltpu.VMEM((5, length, length), BF16),
            square,
            square,
            square,
            square,
            pltpu.VMEM((length, length), F32),
            dma((cols + 6,)),
            dma((steps,)),
            dma((steps,)),
            dma,
            dma,
            dma((steps,)),
            dma((steps,)),
        ],
        compiler_params=pltpu.CompilerParams(
            collective_id=0, has_side_effects=True, vmem_limit_bytes=54 * 2**20
        ),
        name="solve",
    )(
        shift_index,
        shift_table,
        eig_z,
        eig_x.reshape(1, length),
        eig_y.reshape(1, length),
        columns.reshape(cols, cells, length),
        basis_in_x,
        basis_in_y,
        basis_in_z,
        basis_out_x,
        basis_out_y,
        basis_out_z,
    )
    return solved.reshape(columns.shape)


def solution(mesh):
    in_specs = (P(None, "grp", "pen", None), P(), P(), P(), P(), P(), P(), P(), P(), P(), P(), P())
    out_specs = P(None, "grp", "pen", None)
    return jax.shard_map(
        per_device, mesh=mesh, in_specs=in_specs, out_specs=out_specs, check_vma=False
    )
```
